32 devices in a mesh: ctx: 8 (over z, y), fsdp: 4 (over x, core).
Axes of the slice: x: 2, y: 2, z: 4, core: 2. Of those that a mesh axis runs over, the one named last changes fastest.
Arguments:
- hidden: bfloat16 [4, 2048, 576], P('fsdp', 'ctx'), may hold values from -6 to 6
- positions: int32 [4, 2048], P('fsdp', 'ctx'), may hold values from 0 to 2047, as said below
- cotangent: bfloat16 [4, 2048, 576], P('fsdp', 'ctx'), may hold values from -6 to 6
- gain_attn: bfloat16 [576], P('fsdp'), may hold values from 0.5 to 1.5
- gain_mlp: bfloat16 [576], P('fsdp'), may hold values from 0.5 to 1.5
- w_query: bfloat16 [576, 576], P('fsdp'), may hold values from -0.25 to 0.25
- w_key: bfloat16 [576, 192], P('fsdp'), may hold values from -0.25 to 0.25
- w_value: bfloat16 [576, 192], P('fsdp'), may hold values from -0.25 to 0.25
- w_output: bfloat16 [576, 576], P('fsdp'), may hold values from -3 to 3
- w_gate: bfloat16 [576, 1536], P('fsdp'), may hold values from -0.25 to 0.25
- w_up: bfloat16 [576, 1536], P('fsdp'), may hold values from -0.25 to 0.25
- w_down: bfloat16 [1536, 576], P('fsdp'), may hold values from -0.15625 to 0.15625
- moment_gain_attn: float32 [576], P('fsdp'), may hold values from -96 to 96
- moment_gain_mlp: float32 [576], P('fsdp'), may hold values from -96 to 96
- moment_query: float32 [576, 576], P('fsdp'), as said below
- moment_key: float32 [576, 192], P('fsdp'), as said below
- moment_value: float32 [576, 192], P('fsdp'), as said below
- moment_output: float32 [576, 576], P('fsdp'), as said below
- moment_gate: float32 [576, 1536], P('fsdp'), as said below
- moment_up: float32 [576, 1536], P('fsdp'), as said below
- moment_down: float32 [1536, 576], P('fsdp'), as said below
Outputs:
- output: bfloat16 [4, 2048, 576], P('fsdp', 'ctx')
- grad_hidden: float32 [4, 2048, 576], P('fsdp', 'ctx')
- grad_gain_attn: float32 [576], P('fsdp')
- grad_gain_mlp: float32 [576], P('fsdp')
- grad_query: float32 [576, 576], P('fsdp')
- grad_key: float32 [576, 192], P('fsdp')
- grad_value: float32 [576, 192], P('fsdp')
- grad_output: float32 [576, 576], P('fsdp')
- grad_gate: float32 [576, 1536], P('fsdp')
- grad_up: float32 [576, 1536], P('fsdp')
- grad_down: float32 [1536, 576], P('fsdp')
- new_moment_gain_attn: float32 [576], P('fsdp')
- new_moment_gain_mlp: float32 [576], P('fsdp')
- new_moment_query: float32 [576, 576], P('fsdp')
- new_moment_key: float32 [576, 192], P('fsdp')
- new_moment_value: float32 [576, 192], P('fsdp')
- new_moment_output: float32 [576, 576], P('fsdp')
- new_moment_gate: float32 [576, 1536], P('fsdp')
- new_moment_up: float32 [576, 1536], P('fsdp')
- new_moment_down: float32 [1536, 576], P('fsdp')
- new_gain_attn: float32 [576], P('fsdp')
- new_gain_mlp: float32 [576], P('fsdp')
- new_query: float32 [576, 576], P('fsdp')
- new_key: float32 [576, 192], P('fsdp')
- new_value: float32 [576, 192], P('fsdp')
- new_output: float32 [576, 576], P('fsdp')
- new_gate: float32 [576, 1536], P('fsdp')
- new_up: float32 [576, 1536], P('fsdp')
- new_down: float32 [1536, 576], P('fsdp')
The draws below stay inside these ranges and needn't reach their ends.
Inputs may be any that keep to these rules, and one draw needn't show every extreme that they name: For each sequence, its row of positions holds every number of 0 to 2047 exactly once, in runs of 128 consecutive numbers that start at multiples of 128, each run within one device's rows; the order of the runs varies. `moment_query`: momentum of a matrix. `moment_key`: momentum of a matrix. `moment_value`: momentum of a matrix. `moment_output`: momentum of a matrix. `moment_gate`: momentum of a matrix. `moment_up`: momentum of a matrix. `moment_down`: momentum of a matrix.
All inputs are finite; a program needn't handle non-finite values.
Results may differ from the reference program's by a relative error of at most 0.038.
Values may be sent and summed in bfloat16 or wider, within the bound.
No kernel may reach another device: no remote copies, remote signals or barrier semaphores. Data moves between devices by JAX's collectives and lax.ppermute only.
A program may use at most 256 MiB of HBM per device.

```python
import math
import jax
import jax.numpy as jnp
from jax import lax

D = 576
H = 9
KVH = 3
HD = 64
FF = 1536
NEWTON = 5
KV = 192
SPAN = 128
SEQ_ROWS = 2048
SEQS = 4
N_CTX = 8


def draw_positions(key, part):
    runs = SEQ_ROWS // SPAN
    seq_keys = jax.random.split(key, SEQS)

    def one_sequence(seq_key):
        order = jax.random.permutation(seq_key, runs).astype(jnp.int32)
        within = jnp.arange(SPAN, dtype=jnp.int32)
        return (order[:, None] * SPAN + within[None, :]).reshape(SEQ_ROWS).astype(jnp.int32)
    return jax.vmap(one_sequence)(seq_keys)


def moment_matrix(key, label, rows, cols):
    spread = float(N_CTX)
    own_key = jax.random.fold_in(key, label)
    noise = jnp.clip(jax.random.normal(own_key, (rows, cols), jnp.float32), -6.0, 6.0) * spread
    diagonal = (jnp.arange(rows)[:, None] == jnp.arange(cols)[None, :]).astype(jnp.float32)
    return noise + 3.0 * spread * math.sqrt(min(rows, cols)) * diagonal


def draw_moment_query(key, part):
    return moment_matrix(key, 1, D, D)


def draw_moment_key(key, part):
    return moment_matrix(key, 2, D, KV)


def draw_moment_value(key, part):
    return moment_matrix(key, 3, D, KV)


def draw_moment_output(key, part):
    return moment_matrix(key, 4, D, D)


def draw_moment_gate(key, part):
    return moment_matrix(key, 5, D, FF)


def draw_moment_up(key, part):
    return moment_matrix(key, 6, D, FF)


def draw_moment_down(key, part):
    return moment_matrix(key, 7, FF, D)


def level_of(stream_key, shape, pieces, least, top_value):
    factor_of = 1.0
    for dim, parts in pieces:
        steps = jax.random.uniform(jax.random.fold_in(jax.random.fold_in(stream_key, 6), dim), (parts,), jnp.float32, least / len(pieces), top_value / len(pieces))
        factor_of = factor_of * jnp.repeat(jnp.exp(steps), shape[dim] // parts).reshape((-1,) + (1,) * (len(shape) - 1 - dim))
    return factor_of


def scatter_about(key, dims, scale, limit, cuts=(), kind=jnp.bfloat16):
    factor_of = level_of(key, dims, cuts, -0.22, 0.18) if cuts else 1.0
    values = jax.random.normal(key, dims, jnp.float32) * scale * factor_of
    return jnp.minimum(jnp.maximum(values, -limit), limit).astype(kind)


def setup_inputs(seed: int = 0) -> dict:
    seeds = jax.random.split(jax.random.key(seed), 22)
    hidden = scatter_about(seeds[0], (SEQS, SEQ_ROWS, D), 1.0, 6.0, ((0, 4), (1, 8)))
    positions = draw_positions(jax.random.fold_in(seeds[21], 71), 0)
    cotangent = scatter_about(seeds[2], (SEQS, SEQ_ROWS, D), 1.0, 6.0, ((0, 4), (1, 8)))
    gain_attn = jnp.clip(1.0 + 0.1 * jax.random.normal(seeds[3], (D,), jnp.float32), 0.5, 1.5).astype(jnp.bfloat16)
    gain_mlp = jnp.clip(1.0 + 0.1 * jax.random.normal(seeds[4], (D,), jnp.float32), 0.5, 1.5).astype(jnp.bfloat16)
    w_query = scatter_about(seeds[5], (D, D), D ** -0.5, 0.25, ((0, 4),))
    w_key = scatter_about(seeds[6], (D, KV), D ** -0.5, 0.25, ((0, 4),))
    w_value = scatter_about(seeds[7], (D, KV), D ** -0.5, 0.25, ((0, 4),))
    w_output = scatter_about(seeds[8], (D, D), 4 ** -0.5, 3.0, ((0, 4),))
    w_gate = scatter_about(seeds[9], (D, FF), D ** -0.5, 0.25, ((0, 4),))
    w_up = scatter_about(seeds[10], (D, FF), D ** -0.5, 0.25, ((0, 4),))
    w_down = scatter_about(seeds[11], (FF, D), FF ** -0.5, 0.15625, ((0, 4),))
    moment_gain_attn = scatter_about(seeds[12], (D,), (2 * N_CTX), 96.0, ((0, 4),), jnp.float32)
    moment_gain_mlp = scatter_about(seeds[13], (D,), (2 * N_CTX), 96.0, ((0, 4),), jnp.float32)
    moment_query = draw_moment_query(jax.random.fold_in(seeds[21], 71), 0)
    moment_key = draw_moment_key(jax.random.fold_in(seeds[21], 71), 0)
    moment_value = draw_moment_value(jax.random.fold_in(seeds[21], 71), 0)
    moment_output = draw_moment_output(jax.random.fold_in(seeds[21], 71), 0)
    moment_gate = draw_moment_gate(jax.random.fold_in(seeds[21], 71), 0)
    moment_up = draw_moment_up(jax.random.fold_in(seeds[21], 71), 0)
    moment_down = draw_moment_down(jax.random.fold_in(seeds[21], 71), 0)
    return {"hidden": hidden, "positions": positions, "cotangent": cotangent, "gain_attn": gain_attn, "gain_mlp": gain_mlp, "w_query": w_query, "w_key": w_key, "w_value": w_value, "w_output": w_output, "w_gate": w_gate, "w_up": w_up, "w_down": w_down, "moment_gain_attn": moment_gain_attn, "moment_gain_mlp": moment_gain_mlp, "moment_query": moment_query, "moment_key": moment_key, "moment_value": moment_value, "moment_output": moment_output, "moment_gate": moment_gate, "moment_up": moment_up, "moment_down": moment_down}


@jax.custom_vjp
def low(v):
    return lax.optimization_barrier(v.astype(jnp.bfloat16)).astype(jnp.float32)

@jax.custom_vjp
def low_back(v):
    return v

def low_keep(v):
    return (low(v), None)

def low_pass(kept, grad):
    return (grad,)

def back_keep(v):
    return (v, None)

def back_low(kept, grad):
    return (low(grad),)
low.defvjp(low_keep, low_pass)
low_back.defvjp(back_keep, back_low)
epsilon = 1e-05
rope_base = 100000.0
score_scale = 0.125
momentum_decay = 0.95
matrix_rate = 4.0
gain_factor = 0.5
newton_terms = (3.4445, -4.775, 2.0315)
largest_score = lax.Precision.HIGHEST

def angles(positions, head_size):
    halfway = head_size // 2
    inverse = rope_base ** (-(jnp.arange(halfway, dtype=jnp.float32) * 2.0) / head_size)
    phase = positions.astype(jnp.float32)[..., None] * inverse
    return (jnp.cos(phase), jnp.sin(phase))

def rotate(tensor, cosine, sine):
    halfway = tensor.shape[-1] // 2
    first_half = tensor[..., :halfway]
    second_half = tensor[..., halfway:]
    return jnp.concatenate([first_half * cosine - second_half * sine, second_half * cosine + first_half * sine], -1)

def rms_scale(values):
    return lax.rsqrt(lax.optimization_barrier(jnp.mean(values * values, axis=-1, keepdims=True)) + epsilon)

def product(left_operand, right_operand):
    return jnp.einsum('uvm,mn->uvn', left_operand, right_operand, precision=largest_score)

def attend_sequence(inputs):
    queries, keys, values, seq_positions = inputs
    qblock = math.gcd(SEQ_ROWS, 512)
    grouped = queries.reshape(SEQ_ROWS // qblock, qblock, KVH, H // KVH, HD)
    query_pos = seq_positions.reshape(SEQ_ROWS // qblock, qblock)

    @jax.checkpoint
    def one_block(block_inputs):
        query_block, block_pos = block_inputs
        raw_scores = jnp.einsum('tgrd,ngd->tgrn', query_block, keys, precision=largest_score)
        scores = score_scale * low_back(raw_scores)
        allowed = (seq_positions[None, :] <= block_pos[:, None])[:, None, None, :]
        scores = jnp.where(allowed, scores, -1e+30)
        highest_score = lax.optimization_barrier(jnp.max(scores, axis=-1, keepdims=True))
        weights = jnp.where(allowed, jnp.exp(scores - highest_score), 0.0)
        weights = weights / lax.optimization_barrier(jnp.sum(weights, axis=-1, keepdims=True))
        weights = low(weights)
        return jnp.einsum('tgrn,ngd->tgrd', weights, values, precision=largest_score)
    outcome = lax.map(one_block, (grouped, query_pos))
    return outcome.reshape(SEQ_ROWS, H * HD)

def forward(hidden, gain_attn, gain_mlp, w_query, w_key, w_value, w_output, w_gate, w_up, w_down, positions, cosine, sine):
    normed = low(hidden * rms_scale(hidden) * gain_attn)
    query_pre = low_back(product(normed, w_query))
    key_pre = low_back(product(normed, w_key))
    value_pre = low(low_back(product(normed, w_value)))
    query_rot = low(rotate(query_pre.reshape(SEQS, SEQ_ROWS, H, HD), cosine, sine))
    key_rot = low(rotate(key_pre.reshape(SEQS, SEQ_ROWS, KVH, HD), cosine, sine))
    value_heads = value_pre.reshape(SEQS, SEQ_ROWS, KVH, HD)
    attended = lax.map(attend_sequence, (query_rot, key_rot, value_heads, positions))
    attended = low(low_back(attended))
    mixed = hidden + low_back(product(attended, w_output))
    normed_mlp = low(mixed * rms_scale(mixed) * gain_mlp)
    gate_pre = low_back(product(normed_mlp, w_gate))
    up_pre = low_back(product(normed_mlp, w_up))
    inner = low(jax.nn.silu(gate_pre) * up_pre)
    return mixed + low_back(product(inner, w_down))

def orthogonalize(matrix):
    tall = matrix.shape[0] > matrix.shape[1]
    working = matrix.T if tall else matrix
    frobenius = jnp.sqrt(jnp.sum(working * working))
    current = working / (frobenius + 1e-07)
    for sweep in range(NEWTON):
        gram = jnp.dot(current, current.T, precision=largest_score)
        square_gram = jnp.dot(gram, gram, precision=largest_score)
        mixture = newton_terms[1] * gram + newton_terms[2] * square_gram
        current = newton_terms[0] * current + jnp.dot(mixture, current, precision=largest_score)
    return current.T if tall else current

def reference(hidden, positions, cotangent, gain_attn, gain_mlp, w_query, w_key, w_value, w_output, w_gate, w_up, w_down, moment_gain_attn, moment_gain_mlp, moment_query, moment_key, moment_value, moment_output, moment_gate, moment_up, moment_down):
    cosine, sine = angles(positions, HD)
    cosine = cosine[:, :, None, :]
    sine = sine[:, :, None, :]
    params = [hidden, gain_attn, gain_mlp, w_query, w_key, w_value, w_output, w_gate, w_up, w_down]
    params = [entry.astype(jnp.float32) for entry in params]

    def objective(*inputs):
        return forward(*inputs, positions, cosine, sine)
    result, pullback = jax.vjp(objective, *params)
    gradients = pullback(cotangent.astype(jnp.float32))
    output = result.astype(jnp.bfloat16)
    grad_hidden = gradients[0]
    weight_grads = gradients[1:]
    old_weights = params[1:]
    moments = [moment_gain_attn, moment_gain_mlp, moment_query, moment_key, moment_value, moment_output, moment_gate, moment_up, moment_down]
    new_moments = [momentum_decay * old + fresh for old, fresh in zip(moments, weight_grads)]
    gain_step = gain_factor / math.sqrt(float(SEQS * SEQ_ROWS))
    new_weights = [old_weights[0] - gain_step * new_moments[0], old_weights[1] - gain_step * new_moments[1]]
    for matrix, weight in zip(new_moments[2:], old_weights[2:]):
        factor = math.sqrt(max(1.0, float(matrix.shape[1]) / matrix.shape[0]))
        new_weights.append(weight - matrix_rate * factor * orthogonalize(matrix))
    return (output, grad_hidden, weight_grads[0], weight_grads[1], weight_grads[2], weight_grads[3], weight_grads[4], weight_grads[5], weight_grads[6], weight_grads[7], weight_grads[8], new_moments[0], new_moments[1], new_moments[2], new_moments[3], new_moments[4], new_moments[5], new_moments[6], new_moments[7], new_moments[8], new_weights[0], new_weights[1], new_weights[2], new_weights[3], new_weights[4], new_weights[5], new_weights[6], new_weights[7], new_weights[8])
```

```python
import math

import jax
import jax.numpy as jnp
from jax import lax
from jax.experimental import pallas as pl
from jax.experimental.pallas import tpu as pltpu
from jax.sharding import PartitionSpec as P

D = 576
H = 9
KVH = 3
HD = 64
FF = 1536
NEWTON = 5
KV = 192


epsilon = 1e-05
rope_base = 100000.0
score_scale = 0.125
momentum_decay = 0.95
matrix_rate = 4.0
gain_factor = 0.5
newton_terms = (3.4445, -4.775, 2.0315)
minimum_floor = -1e30
low = jnp.bfloat16
wide = jnp.float32


def angles(positions, head_size):
    halfway = head_size // 2
    inverse = rope_base ** (-(jnp.arange(halfway, dtype=jnp.float32) * 2.0) / head_size)
    phase = positions.astype(jnp.float32)[..., None] * inverse
    return (jnp.cos(phase), jnp.sin(phase))


def rotate(tensor, cosine, sine):
    halfway = tensor.shape[-1] // 2
    first_half = tensor[..., :halfway]
    second_half = tensor[..., halfway:]
    return jnp.concatenate(
        [first_half * cosine - second_half * sine, second_half * cosine + first_half * sine], -1
    )


def unrotate(tensor, cosine, sine):
    halfway = tensor.shape[-1] // 2
    first_half = tensor[..., :halfway]
    second_half = tensor[..., halfway:]
    return jnp.concatenate(
        [first_half * cosine + second_half * sine, second_half * cosine - first_half * sine], -1
    )


def over_blocks(function, running, rows_kv, rows_pos):
    row_count = rows_kv.shape[0]
    width = math.gcd(row_count, 1024)

    def step_forward(carried, block_index):
        first_row = block_index * width
        block_kv = lax.dynamic_slice_in_dim(rows_kv, first_row, width)
        block_pos = lax.dynamic_slice_in_dim(rows_pos, first_row, width)
        return (function(carried, block_kv, block_pos), None)

    finished, unused = lax.scan(step_forward, running, jnp.arange(row_count // width))
    return finished


def across(value, axis, bit):
    size = lax.axis_size(axis)
    return lax.ppermute(value, axis, [(i, i ^ bit) for i in range(size)])


def pick(array, index, axis):
    return lax.dynamic_index_in_dim(array, index, axis, keepdims=False)


def in_order(bit, mine, theirs, axis=0):
    first = jnp.where(bit == 0, mine, theirs)
    second = jnp.where(bit == 0, theirs, mine)
    return jnp.stack([first, second], axis)


def gather_shards(shard):
    place = lax.axis_index("fsdp")
    pair = in_order(place // 2, shard, across(shard, "fsdp", 2))
    both = in_order(place % 2, pair, across(pair, "fsdp", 1), 1)
    return both.reshape((4,) + shard.shape)


def exchange(blocks):
    place = lax.axis_index("fsdp")
    far, near = place // 2, place % 2
    grid = blocks.reshape((2, 2) + blocks.shape[1:])
    came = across(pick(grid, 1 - far, 0), "fsdp", 2)
    rows = in_order(far, pick(grid, far, 0), came)
    came = across(pick(rows, 1 - near, 1), "fsdp", 1)
    both = in_order(near, pick(rows, near, 1), came, 1)
    return both.reshape(blocks.shape)


def gather_context(block):
    bit = lax.axis_size("ctx") // 2
    while bit:
        block = jnp.concatenate([block, across(block, "ctx", bit)], 0)
        bit //= 2
    return block


def scatter_context(terms):
    bit = 1
    while bit < lax.axis_size("ctx"):
        half = terms.shape[0] // 2
        came = across(terms[half:].astype(low), "ctx", bit)
        terms = terms[:half] + came.astype(wide)
        bit *= 2
    return terms


def add(mine, came):
    return (mine.astype(wide) + came.astype(wide)).astype(low)


def reduce_context(array, halvings):
    place = lax.axis_index("ctx")
    size = lax.axis_size("ctx")
    rows = array.shape[0]
    bits = []
    bit = 1
    while bit < size:
        if len(bits) < halvings:
            mine = (place // bit) % 2
            pair = array.reshape((2, array.shape[0] // 2) + array.shape[1:])
            array = add(pick(pair, mine, 0), across(pick(pair, 1 - mine, 0), "ctx", bit))
            bits.append(bit)
        else:
            array = add(array, across(array, "ctx", bit))
        bit *= 2
    for bit in reversed(bits):
        pair = in_order((place // bit) % 2, array, across(array, "ctx", bit))
        array = pair.reshape((-1,) + array.shape[1:])
    return array


def newton_step(current, tall):
    dims = (((0,), (0,)), ((), ())) if tall else (((1,), (1,)), ((), ()))
    rounded = current.astype(low)
    gram = lax.dot_general(rounded, rounded, dims, preferred_element_type=wide)
    count = gram.shape[0]
    diagonal = lax.broadcasted_iota(jnp.int32, gram.shape, 0) == lax.broadcasted_iota(
        jnp.int32, gram.shape, 1
    )
    level = jnp.sum(jnp.where(diagonal, gram, 0.0), keepdims=True) / count
    rest = jnp.where(diagonal, gram - level, gram)
    rest_low = rest.astype(low)
    square = jnp.dot(rest_low, rest_low, preferred_element_type=wide)
    square_level = jnp.sum(jnp.where(diagonal, square, 0.0), keepdims=True) / count
    square_rest = jnp.where(diagonal, square - square_level, square)
    first, second, third = newton_terms
    mixture = (second + 2.0 * third * level) * rest + third * square_rest
    shift = first + second * level + third * (level * level + square_level)
    mixture_low = mixture.astype(low)
    if tall:
        turned = jnp.dot(rounded, mixture_low, preferred_element_type=wide)
    else:
        turned = jnp.dot(mixture_low, rounded, preferred_element_type=wide)
    return shift * current + turned


def newton_kernel(*refs):
    count = len(refs) // 3
    sources, results, states = refs[:count], refs[count : 2 * count], refs[2 * count :]
    for source, state in zip(sources, states):
        matrix = source[...]
        norm = jnp.sqrt(jnp.sum(matrix * matrix, keepdims=True))
        state[...] = matrix / (norm + 1e-07)

    def sweep(index, carried):
        for state in states:
            state[...] = newton_step(state[...], state.shape[0] > state.shape[1])
        return carried

    lax.fori_loop(0, NEWTON, sweep, 0)
    for result, state in zip(results, states):
        result[...] = state[...].astype(result.dtype)


def orthogonalize(*matrices):
    return pl.pallas_call(
        newton_kernel,
        out_shape=[jax.ShapeDtypeStruct(m.shape, low) for m in matrices],
        scratch_shapes=[pltpu.VMEM(m.shape, wide) for m in matrices],
        name="newton",
    )(*matrices)


def columns_to_rows(shard):
    turned = shard.T
    rows = D // 4
    return jnp.concatenate([turned[i * rows : (i + 1) * rows] for i in range(4)], 1)


def rows_to_columns(packed):
    wide_part = FF // 4
    return jnp.concatenate(
        [packed[:, i * wide_part : (i + 1) * wide_part] for i in range(4)], 0
    ).T


def swap_blocks(blocks):
    part = FF // 4
    rows = [
        jnp.concatenate([blocks[s, :, j * part : (j + 1) * part] for s in range(4)], 1)
        for j in range(4)
    ]
    return jnp.stack(rows)


def per_device(
    hidden,
    positions,
    cotangent,
    gain_attn,
    gain_mlp,
    w_query,
    w_key,
    w_value,
    w_output,
    w_gate,
    w_up,
    w_down,
    moment_gain_attn,
    moment_gain_mlp,
    moment_query,
    moment_key,
    moment_value,
    moment_output,
    moment_gate,
    moment_up,
    moment_down,
):
    place = lax.axis_index("fsdp")
    far, near = place // 2, place % 2
    shard_rows = D // 4
    gains = jnp.stack([gain_attn, gain_mlp])
    gain_rows = jnp.pad(gains, ((0, 6), (0, 1024 - shard_rows)))
    pack_qkv = jnp.concatenate(
        [jnp.pad(jnp.concatenate([w_query, w_key, w_value], 1), ((0, 0), (0, 64))), gain_rows], 0
    )
    all_qkv = gather_shards(pack_qkv)
    full_qkv = all_qkv[:, :shard_rows].reshape(D, 1024)
    gain_first = all_qkv[:, shard_rows, :shard_rows].reshape(D).astype(wide)
    gain_second = all_qkv[:, shard_rows + 1, :shard_rows].reshape(D).astype(wide)
    full_rest = gather_shards(jnp.concatenate([w_gate, w_up, w_output], 1)).reshape(D, -1)
    full_gate_up = full_rest[:, : 2 * FF]
    full_output = full_rest[:, 2 * FF :]
    full_down = gather_shards(w_down).reshape(FF, D)
    groups = H // KVH
    tokens = hidden.shape[1]
    features = hidden[0].astype(wide)
    local_pos = positions[0]
    all_pos = gather_context(local_pos.reshape(-1, 128)).reshape(-1)
    sequence_length = all_pos.shape[0]
    cosine, sine = angles(local_pos, HD)
    cosine = cosine[:, None, :]
    sine = sine[:, None, :]
    scale_first = lax.rsqrt(jnp.mean(features * features, axis=-1, keepdims=True) + epsilon)
    normed = (features * scale_first * gain_first).astype(low)
    qkv_pre = jnp.dot(normed, full_qkv, preferred_element_type=wide)
    query_pre = qkv_pre[:, :D]
    key_pre = qkv_pre[:, D : D + KV]
    value_pre = qkv_pre[:, D + KV : D + 2 * KV]
    query_rot = rotate(query_pre.reshape(tokens, H, HD), cosine, sine).astype(low)
    key_rot = rotate(key_pre.reshape(tokens, KVH, HD), cosine, sine).astype(low).reshape(tokens, KV)
    key_value = jnp.concatenate([key_rot, value_pre.astype(low)], 1)
    query_grouped = query_rot.reshape(tokens, KVH, groups, HD)
    all_kv = gather_context(key_value)

    def scores_of(block_kv, block_pos):
        block_keys = block_kv[:, :KV].reshape(-1, KVH, HD)
        raw_scores = jnp.einsum(
            "tgrd,ngd->tgrn", query_grouped, block_keys, preferred_element_type=jnp.float32
        )
        allowed = (block_pos[None, :] <= local_pos[:, None])[:, None, None, :]
        return (score_scale * raw_scores, allowed)

    def block_forward_pass(running, block_kv, block_pos):
        peak, summed, accum = running
        scores, allowed = scores_of(block_kv, block_pos)
        masked = jnp.where(allowed, scores, minimum_floor)
        new_peak = jnp.maximum(peak, jnp.max(masked, axis=-1))
        factor = jnp.exp(peak - new_peak)
        weights = jnp.where(allowed, jnp.exp(scores - new_peak[..., None]), 0.0)
        block_values = block_kv[:, KV:].reshape(-1, KVH, HD)
        accum = accum * factor[..., None] + jnp.einsum(
            "tgrn,ngd->tgrd",
            weights.astype(jnp.bfloat16),
            block_values,
            preferred_element_type=jnp.float32,
        )
        summed = summed * factor + jnp.sum(weights, axis=-1)
        return (new_peak, summed, accum)

    initial = (
        jnp.full((tokens, KVH, groups), minimum_floor, jnp.float32),
        jnp.zeros((tokens, KVH, groups), jnp.float32),
        jnp.zeros((tokens, KVH, groups, HD), jnp.float32),
    )
    running = over_blocks(
        block_forward_pass, initial, all_kv, all_pos
    )
    peak, summed, accum = running
    attended = accum / summed[..., None]
    log_total = peak + jnp.log(summed)
    attended_low = attended.reshape(tokens, D).astype(low)
    mixed = features + jnp.dot(attended_low, full_output, preferred_element_type=wide)
    second_scale = lax.rsqrt(jnp.mean(mixed * mixed, axis=-1, keepdims=True) + epsilon)
    normed_mlp = (mixed * second_scale * gain_second).astype(low)
    gate_up = jnp.dot(normed_mlp, full_gate_up, preferred_element_type=wide)
    gate_pre = gate_up[:, :FF]
    up_pre = gate_up[:, FF:]
    inner = (jax.nn.silu(gate_pre) * up_pre).astype(low)
    result = mixed + jnp.dot(inner, full_down, preferred_element_type=wide)
    output = result.astype(low)[None]
    upstream_low = cotangent[0]
    upstream = upstream_low.astype(wide)
    grad_inner = jnp.einsum("td,fd->tf", upstream_low, full_down, preferred_element_type=wide)
    sigma = jax.nn.sigmoid(gate_pre)
    grad_up_pre = (grad_inner * gate_pre * sigma).astype(low)
    grad_gate_pre = (grad_inner * up_pre * sigma * (1.0 + gate_pre * (1.0 - sigma))).astype(low)
    grad_pre = jnp.concatenate([grad_gate_pre, grad_up_pre], 1)
    grad_normed_mlp = jnp.einsum("tf,df->td", grad_pre, full_gate_up, preferred_element_type=wide)
    gain_term_mlp = (grad_normed_mlp * mixed * second_scale).astype(low)
    inner_second = grad_normed_mlp * gain_second
    grad_mixed = (
        upstream
        + second_scale * inner_second
        - mixed * second_scale**3 * jnp.mean(inner_second * mixed, axis=-1, keepdims=True)
    )
    mixed_low = grad_mixed.astype(low)
    grad_gate_up = jnp.einsum("td,tf->df", normed_mlp, grad_pre, preferred_element_type=wide)
    grad_gate_up = grad_gate_up.astype(low)
    turned_down = jnp.einsum("td,tf->df", upstream_low, inner, preferred_element_type=wide)
    grad_out = jnp.einsum("td,te->de", attended_low, mixed_low, preferred_element_type=wide)
    even = jnp.stack([grad_gate_up[:, :FF], turned_down.astype(low)])
    odd = jnp.stack([grad_gate_up[:, FF:], jnp.pad(grad_out.astype(low), ((0, 0), (0, FF - D)))])
    kept = jnp.where(near == 0, even, odd)
    sent = jnp.where(near == 0, odd, even)
    chip = add(kept, across(sent, "fsdp", 1))
    own = add(pick(chip, far, 0), across(pick(chip, 1 - far, 0), "fsdp", 2))
    own_grad = reduce_context(own, 2)
    is_down = place == 2

    def by_shard(matrix):
        blocks = matrix.reshape(4, shard_rows, FF)
        return jnp.where(is_down, swap_blocks(blocks), blocks)

    moments_out = jnp.stack(
        [
            moment_gate.astype(low),
            moment_up.astype(low),
            columns_to_rows(moment_down.astype(low)),
            jnp.pad(moment_output.astype(low), ((0, 0), (0, FF - D))),
        ]
    )
    own_old = exchange(moments_out)
    own_old = jnp.where(is_down, swap_blocks(own_old), own_old).reshape(D, FF)
    own_moment = momentum_decay * own_old.astype(wide) + own_grad.astype(wide)
    (own_orthogonal,) = orthogonalize(own_moment)
    grads_back = exchange(by_shard(own_grad))
    steps_back = exchange(by_shard(own_orthogonal))

    grad_attended = jnp.einsum("te,de->td", mixed_low, full_output, preferred_element_type=wide)
    grad_attended = grad_attended.astype(low)
    grad_grouped = grad_attended.reshape(tokens, KVH, groups, HD)
    delta = jnp.sum(grad_grouped.astype(wide) * attended, axis=-1)
    backward_kv = all_kv
    width = math.gcd(sequence_length, 1024)

    def backward_block(grad_query_rot, block_index):
        first_row = block_index * width
        block_kv = lax.dynamic_slice_in_dim(backward_kv, first_row, width)
        block_pos = lax.dynamic_slice_in_dim(all_pos, first_row, width)
        scores, allowed = scores_of(block_kv, block_pos)
        weights = jnp.where(allowed, jnp.exp(scores - log_total[..., None]), 0.0)
        block_keys = block_kv[:, :KV].reshape(-1, KVH, HD)
        block_values = block_kv[:, KV:].reshape(-1, KVH, HD)
        grad_weights = jnp.einsum(
            "tgrd,ngd->tgrn", grad_grouped, block_values, preferred_element_type=jnp.float32
        )
        grad_scores = (score_scale * weights * (grad_weights - delta[..., None])).astype(
            jnp.bfloat16
        )
        grad_query_rot = grad_query_rot + jnp.einsum(
            "tgrn,ngd->tgrd", grad_scores, block_keys, preferred_element_type=jnp.float32
        )
        key_term = jnp.einsum(
            "tgrn,tgrd->ngd", grad_scores, query_grouped, preferred_element_type=jnp.float32
        ).reshape(width, KV)
        value_term = jnp.einsum(
            "tgrn,tgrd->ngd",
            weights.astype(jnp.bfloat16),
            grad_grouped,
            preferred_element_type=jnp.float32,
        ).reshape(width, KV)
        return (grad_query_rot, jnp.concatenate([key_term, value_term], 1))

    grad_query_rot, terms = lax.scan(
        backward_block,
        jnp.zeros((tokens, KVH, groups, HD), jnp.float32),
        jnp.arange(sequence_length // width),
    )
    terms = terms.reshape(sequence_length, 2 * KV)
    key_grads = scatter_context(terms)
    grad_query_pre = unrotate(grad_query_rot.reshape(tokens, H, HD), cosine, sine)
    grad_key_pre = unrotate(key_grads[:, :KV].reshape(tokens, KVH, HD), cosine, sine)
    grad_qkv_pre = jnp.concatenate(
        [
            grad_query_pre.reshape(tokens, D).astype(low),
            grad_key_pre.reshape(tokens, KV).astype(low),
            key_grads[:, KV:].astype(low),
        ],
        1,
    )
    grad_normed = jnp.einsum(
        "te,de->td", grad_qkv_pre, full_qkv[:, : D + 2 * KV], preferred_element_type=wide
    )
    inner_first = grad_normed * gain_first
    grad_hidden = (
        grad_mixed
        + scale_first * inner_first
        - features * scale_first**3 * jnp.mean(inner_first * features, axis=-1, keepdims=True)
    )
    gain_term = (grad_normed * features * scale_first).astype(low)
    ones = jnp.ones((tokens, 32), low)
    grad_qkv = jnp.concatenate(
        [
            jnp.einsum("td,te->de", normed, grad_qkv_pre, preferred_element_type=wide),
            jnp.einsum("td,te->de", gain_term, ones, preferred_element_type=wide),
            jnp.einsum("td,te->de", gain_term_mlp, ones, preferred_element_type=wide),
        ],
        1,
    ).astype(low)
    grid = grad_qkv.reshape(2, 2, shard_rows, 1024)
    chip_qkv = add(pick(grid, near, 1), across(pick(grid, 1 - near, 1), "fsdp", 1))
    own_qkv = add(pick(chip_qkv, far, 0), across(pick(chip_qkv, 1 - far, 0), "fsdp", 2))
    total_qkv = reduce_context(own_qkv, 1).astype(wide)

    def square_part(packed):
        return packed[:, :D]

    total_query = total_qkv[:, :D]
    total_key = total_qkv[:, D : D + KV]
    total_value = total_qkv[:, D + KV : D + 2 * KV]
    total_gain_attn = total_qkv[:, D + 2 * KV]
    total_gain_mlp = total_qkv[:, D + 2 * KV + 32]
    total_grads = (
        total_gain_attn,
        total_gain_mlp,
        total_query,
        total_key,
        total_value,
        square_part(grads_back[3]).astype(wide),
        grads_back[0].astype(wide),
        grads_back[1].astype(wide),
        rows_to_columns(grads_back[2]).astype(wide),
    )
    old_moments = (
        moment_gain_attn,
        moment_gain_mlp,
        moment_query,
        moment_key,
        moment_value,
        moment_output,
        moment_gate,
        moment_up,
        moment_down,
    )
    new_moments = tuple(
        (momentum_decay * old + fresh for old, fresh in zip(old_moments, total_grads))
    )
    small = jnp.concatenate([new_moments[2], new_moments[3], new_moments[4]], 1).astype(low)
    small = jnp.pad(small, ((0, 0), (0, 64)))
    small = gather_shards(small).reshape(D, 1024).astype(wide)
    orthogonal_small = orthogonalize(
        small[:, :D], small[:, D : D + KV], small[:, D + KV : D + 2 * KV]
    )

    def rows_of(matrix):
        return lax.dynamic_slice_in_dim(matrix, place * shard_rows, shard_rows, 0)

    def stepped(weight, values, rows_total, cols_total):
        factor = math.sqrt(max(1.0, float(cols_total) / rows_total))
        return weight.astype(wide) - matrix_rate * factor * values.astype(wide)

    new_gate = stepped(w_gate, steps_back[0], D, FF)
    new_up = stepped(w_up, steps_back[1], D, FF)
    new_down = stepped(w_down, rows_to_columns(steps_back[2]), FF, D)
    new_output = stepped(w_output, square_part(steps_back[3]), D, D)
    new_query = stepped(w_query, rows_of(orthogonal_small[0]), D, D)
    new_key = stepped(w_key, rows_of(orthogonal_small[1]), D, KV)
    new_value = stepped(w_value, rows_of(orthogonal_small[2]), D, KV)
    gain_step = gain_factor / math.sqrt(float(sequence_length * lax.axis_size("fsdp")))
    new_gain_attn = gain_attn.astype(wide) - gain_step * new_moments[0]
    new_gain_mlp = gain_mlp.astype(wide) - gain_step * new_moments[1]
    return (
        output,
        grad_hidden[None],
        *total_grads,
        *new_moments,
        new_gain_attn,
        new_gain_mlp,
        new_query,
        new_key,
        new_value,
        new_output,
        new_gate,
        new_up,
        new_down,
    )


def solution(mesh):
    return jax.shard_map(
        per_device,
        mesh=mesh,
        in_specs=(
            P("fsdp", "ctx", None),
            P("fsdp", "ctx"),
            P("fsdp", "ctx", None),
            P("fsdp"),
            P("fsdp"),
            P("fsdp", None),
            P("fsdp", None),
            P("fsdp", None),
            P("fsdp", None),
            P("fsdp", None),
            P("fsdp", None),
            P("fsdp", None),
            P("fsdp"),
            P("fsdp"),
            P("fsdp", None),
            P("fsdp", None),
            P("fsdp", None),
            P("fsdp", None),
            P("fsdp", None),
            P("fsdp", None),
            P("fsdp", None),
        ),
        out_specs=(
            P("fsdp", "ctx", None),
            P("fsdp", "ctx", None),
            P("fsdp"),
            P("fsdp"),
            P("fsdp", None),
            P("fsdp", None),
            P("fsdp", None),
            P("fsdp", None),
            P("fsdp", None),
            P("fsdp", None),
            P("fsdp", None),
            P("fsdp"),
            P("fsdp"),
            P("fsdp", None),
            P("fsdp", None),
            P("fsdp", None),
            P("fsdp", None),
            P("fsdp", None),
            P("fsdp", None),
            P("fsdp", None),
            P("fsdp"),
            P("fsdp"),
            P("fsdp", None),
            P("fsdp", None),
            P("fsdp", None),
            P("fsdp", None),
            P("fsdp", None),
            P("fsdp", None),
            P("fsdp", None),
        ),
        check_vma=False,
    )
```

```python
import math

import jax
import jax.numpy as jnp
from jax import lax
from jax.experimental import pallas as pl
from jax.experimental.pallas import tpu as pltpu
from jax.sharding import PartitionSpec as P

D = 576
H = 9
KVH = 3
HD = 64
FF = 1536
NEWTON = 5
KV = 192


epsilon = 1e-05
rope_base = 100000.0
score_scale = 0.125
momentum_decay = 0.95
matrix_rate = 4.0
gain_factor = 0.5
newton_terms = (3.4445, -4.775, 2.0315)
minimum_floor = -1e30
low = jnp.bfloat16
wide = jnp.float32


def angles(positions, head_size):
    halfway = head_size // 2
    inverse = rope_base ** (-(jnp.arange(halfway, dtype=jnp.float32) * 2.0) / head_size)
    phase = positions.astype(jnp.float32)[..., None] * inverse
    return (jnp.cos(phase), jnp.sin(phase))


def rotate(tensor, cosine, sine):
    halfway = tensor.shape[-1] // 2
    first_half = tensor[..., :halfway]
    second_half = tensor[..., halfway:]
    return jnp.concatenate(
        [first_half * cosine - second_half * sine, second_half * cosine + first_half * sine], -1
    )


def unrotate(tensor, cosine, sine):
    halfway = tensor.shape[-1] // 2
    first_half = tensor[..., :halfway]
    second_half = tensor[..., halfway:]
    return jnp.concatenate(
        [first_half * cosine + second_half * sine, second_half * cosine - first_half * sine], -1
    )


def across(value, axis, bit):
    size = lax.axis_size(axis)
    return lax.ppermute(value, axis, [(i, i ^ bit) for i in range(size)])


def pick(array, index, axis):
    return lax.dynamic_index_in_dim(array, index, axis, keepdims=False)


def in_order(bit, mine, theirs, axis=0):
    first = jnp.where(bit == 0, mine, theirs)
    second = jnp.where(bit == 0, theirs, mine)
    return jnp.stack([first, second], axis)


def gather_shards(shard, came=None):
    place = lax.axis_index("fsdp")
    came = across(shard, "fsdp", 2) if came is None else came
    pair = in_order(place // 2, shard, came)
    both = in_order(place % 2, pair, across(pair, "fsdp", 1), 1)
    return both.reshape((4,) + shard.shape)


def exchange(blocks):
    place = lax.axis_index("fsdp")
    far, near = place // 2, place % 2
    grid = blocks.reshape((2, 2) + blocks.shape[1:])
    came = across(pick(grid, 1 - far, 0), "fsdp", 2)
    rows = in_order(far, pick(grid, far, 0), came)
    came = across(pick(rows, 1 - near, 1), "fsdp", 1)
    both = in_order(near, pick(rows, near, 1), came, 1)
    return both.reshape(blocks.shape)


def gather_context(block):
    bit = lax.axis_size("ctx") // 2
    while bit > 1:
        block = jnp.concatenate([block, across(block, "ctx", bit)], 0)
        bit //= 2
    return block, across(block, "ctx", 1)


def scatter_context(first, came):
    terms = first.astype(wide) + came.astype(wide)
    bit = 2
    while bit < lax.axis_size("ctx"):
        half = terms.shape[0] // 2
        came = across(terms[half:].astype(low), "ctx", bit)
        terms = terms[:half] + came.astype(wide)
        bit *= 2
    return terms


def add(mine, came):
    return (mine.astype(wide) + came.astype(wide)).astype(low)


def reduce_context(array, halvings):
    place = lax.axis_index("ctx")
    size = lax.axis_size("ctx")
    rows = array.shape[0]
    bits = []
    bit = 1
    while bit < size:
        if len(bits) < halvings:
            mine = (place // bit) % 2
            pair = array.reshape((2, array.shape[0] // 2) + array.shape[1:])
            array = add(pick(pair, mine, 0), across(pick(pair, 1 - mine, 0), "ctx", bit))
            bits.append(bit)
        else:
            array = add(array, across(array, "ctx", bit))
        bit *= 2
    for bit in reversed(bits):
        pair = in_order((place // bit) % 2, array, across(array, "ctx", bit))
        array = pair.reshape((-1,) + array.shape[1:])
    return array


def reduce_rows(matrix):
    place = lax.axis_index("fsdp")
    far, near = place // 2, place % 2
    grid = matrix.reshape(2, 2, matrix.shape[0] // 4, matrix.shape[1])
    chip = add(pick(grid, near, 1), across(pick(grid, 1 - near, 1), "fsdp", 1))
    own = add(pick(chip, far, 0), across(pick(chip, 1 - far, 0), "fsdp", 2))
    return reduce_context(own, 1).astype(wide)


def newton_step(current, tall):
    dims = (((0,), (0,)), ((), ())) if tall else (((1,), (1,)), ((), ()))
    rounded = current.astype(low)
    gram = lax.dot_general(rounded, rounded, dims, preferred_element_type=wide)
    count = gram.shape[0]
    diagonal = lax.broadcasted_iota(jnp.int32, gram.shape, 0) == lax.broadcasted_iota(
        jnp.int32, gram.shape, 1
    )
    level = jnp.sum(jnp.where(diagonal, gram, 0.0), keepdims=True) / count
    rest = jnp.where(diagonal, gram - level, gram)
    rest_low = rest.astype(low)
    square = jnp.dot(rest_low, rest_low, preferred_element_type=wide)
    square_level = jnp.sum(jnp.where(diagonal, square, 0.0), keepdims=True) / count
    square_rest = jnp.where(diagonal, square - square_level, square)
    first, second, third = newton_terms
    mixture = (second + 2.0 * third * level) * rest + third * square_rest
    shift = first + second * level + third * (level * level + square_level)
    mixture_low = mixture.astype(low)
    if tall:
        turned = jnp.dot(rounded, mixture_low, preferred_element_type=wide)
    else:
        turned = jnp.dot(mixture_low, rounded, preferred_element_type=wide)
    return shift * current + turned


def newton_kernel(*refs):
    count = len(refs) // 3
    sources, results, states = refs[:count], refs[count : 2 * count], refs[2 * count :]
    for source, state in zip(sources, states):
        matrix = source[...]
        norm = jnp.sqrt(jnp.sum(matrix * matrix, keepdims=True))
        state[...] = matrix / (norm + 1e-07)

    def sweep(index, carried):
        for state in states:
            state[...] = newton_step(state[...], state.shape[0] > state.shape[1])
        return carried

    lax.fori_loop(0, NEWTON, sweep, 0)
    for result, state in zip(results, states):
        result[...] = state[...].astype(result.dtype)


def orthogonalize(*matrices):
    return pl.pallas_call(
        newton_kernel,
        out_shape=[jax.ShapeDtypeStruct(m.shape, low) for m in matrices],
        scratch_shapes=[pltpu.VMEM(m.shape, wide) for m in matrices],
        name="newton",
    )(*matrices)


KEY_BLOCK = 512


def head_rows(ref, group):
    groups = H // KVH
    return jnp.concatenate(
        [ref[:, h * HD : (h + 1) * HD] for h in range(group * groups, (group + 1) * groups)], 0
    )


def store_heads(ref, group, rows):
    groups = H // KVH
    tokens = ref.shape[0]
    for i in range(groups):
        h = group * groups + i
        ref[:, h * HD : (h + 1) * HD] = rows[i * tokens : (i + 1) * tokens].astype(ref.dtype)


def contract(left, right, left_dim, right_dim):
    return lax.dot_general(
        left, right, (((left_dim,), (right_dim,)), ((), ())), preferred_element_type=wide
    )


def key_rows(ref, start, length, column):
    return ref[pl.ds(start, length), column : column + HD]


def attend_kernel(last, *refs):
    query_ref, kv_ref, query_pos_ref, key_pos_ref = refs[:4]
    if last:
        peak_in, sum_in, accum_in, low_out, attended_out, log_out = refs[4:]
    else:
        peak_out, sum_out, accum_out = refs[4:]
    rows = kv_ref.shape[0]
    block = math.gcd(rows, KEY_BLOCK)
    query_pos = query_pos_ref[...]
    for group in range(KVH):
        queries = head_rows(query_ref, group)

        def step(index, carried):
            peak, summed, accum = carried
            start = pl.multiple_of(index * block, block)
            keys = key_rows(kv_ref, start, block, group * HD)
            values = key_rows(kv_ref, start, block, KV + group * HD)
            scores = score_scale * contract(keys, queries, 1, 1)
            allowed = key_pos_ref[pl.ds(start, block), :] <= query_pos
            masked = jnp.where(allowed, scores, minimum_floor)
            new_peak = jnp.maximum(peak, jnp.max(masked, axis=0, keepdims=True))
            factor = jnp.exp(peak - new_peak)
            weights = jnp.where(allowed, jnp.exp(masked - new_peak), 0.0)
            summed = summed * factor + jnp.sum(weights, axis=0, keepdims=True)
            accum = accum * factor + contract(values, weights.astype(low), 0, 0)
            return (new_peak, summed, accum)

        count = queries.shape[0]
        if last:
            state = (peak_in[group], sum_in[group], accum_in[group])
        else:
            state = (
                jnp.full((1, count), minimum_floor, wide),
                jnp.zeros((1, count), wide),
                jnp.zeros((HD, count), wide),
            )
        peak, summed, accum = lax.fori_loop(0, rows // block, step, state)
        if last:
            attended = accum / summed
            attended_out[group] = attended
            log_out[group] = peak + jnp.log(summed)
            store_heads(low_out, group, attended.T)
        else:
            peak_out[group] = peak
            sum_out[group] = summed
            accum_out[group] = accum


def attend(query, kv, query_pos, key_pos, state=None):
    tokens = query.shape[0]
    count = tokens * (H // KVH)
    row = jax.ShapeDtypeStruct((KVH, 1, count), wide)
    block = jax.ShapeDtypeStruct((KVH, HD, count), wide)
    if state is None:
        shapes = [row, row, block]
    else:
        shapes = [jax.ShapeDtypeStruct((tokens, D), low), block, row]
    return pl.pallas_call(
        lambda *refs: attend_kernel(state is not None, *refs), out_shape=shapes, name="attend"
    )(query, kv, query_pos, key_pos, *(state or ()))


def attend_back_kernel(last, *refs):
    query_ref, grad_ref, attended_ref, log_ref, kv_ref, query_pos_ref, key_pos_ref = refs[:7]
    if last:
        grad_in, grad_query_out, grad_kv_out = refs[7:]
    else:
        grad_query_out, grad_kv_out = refs[7:]
    rows = kv_ref.shape[0]
    block = math.gcd(rows, KEY_BLOCK)
    query_pos = query_pos_ref[...]
    for group in range(KVH):
        queries = head_rows(query_ref, group)
        grads = head_rows(grad_ref, group)
        delta = jnp.sum(grads.astype(wide).T * attended_ref[group], axis=0, keepdims=True)
        log_total = log_ref[group]

        def step(index, grad_query):
            start = pl.multiple_of(index * block, block)
            keys = key_rows(kv_ref, start, block, group * HD)
            values = key_rows(kv_ref, start, block, KV + group * HD)
            scores = score_scale * contract(keys, queries, 1, 1)
            allowed = key_pos_ref[pl.ds(start, block), :] <= query_pos
            masked = jnp.where(allowed, scores, minimum_floor)
            weights = jnp.exp(masked - log_total)
            grad_weights = contract(values, grads, 1, 1)
            grad_scores = (score_scale * weights * (grad_weights - delta)).astype(low)
            key_term = contract(grad_scores, queries, 1, 0)
            value_term = contract(weights.astype(low), grads, 1, 0)
            span = pl.ds(start, block)
            grad_kv_out[span, group * HD : (group + 1) * HD] = key_term.astype(low)
            grad_kv_out[span, KV + group * HD : KV + (group + 1) * HD] = value_term.astype(low)
            return grad_query + contract(keys, grad_scores, 0, 0)

        begin = grad_in[group] if last else jnp.zeros((HD, queries.shape[0]), wide)
        finished = lax.fori_loop(0, rows // block, step, begin)
        if last:
            store_heads(grad_query_out, group, finished.T)
        else:
            grad_query_out[group] = finished


def attend_back(query, grads, attended, logs, kv, query_pos, key_pos, begun=None):
    tokens = query.shape[0]
    count = tokens * (H // KVH)
    if begun is None:
        first = jax.ShapeDtypeStruct((KVH, HD, count), wide)
    else:
        first = jax.ShapeDtypeStruct((tokens, D), wide)
    return pl.pallas_call(
        lambda *refs: attend_back_kernel(begun is not None, *refs),
        out_shape=[first, jax.ShapeDtypeStruct(kv.shape, low)],
        name="attend_back",
    )(query, grads, attended, logs, kv, query_pos, key_pos, *(() if begun is None else (begun,)))


def columns_to_rows(shard):
    turned = shard.T
    rows = D // 4
    return jnp.concatenate([turned[i * rows : (i + 1) * rows] for i in range(4)], 1)


def rows_to_columns(packed):
    wide_part = FF // 4
    return jnp.concatenate(
        [packed[:, i * wide_part : (i + 1) * wide_part] for i in range(4)], 0
    ).T


def swap_blocks(blocks):
    part = FF // 4
    rows = [
        jnp.concatenate([blocks[s, :, j * part : (j + 1) * part] for s in range(4)], 1)
        for j in range(4)
    ]
    return jnp.stack(rows)


def per_device(
    hidden,
    positions,
    cotangent,
    gain_attn,
    gain_mlp,
    w_query,
    w_key,
    w_value,
    w_output,
    w_gate,
    w_up,
    w_down,
    moment_gain_attn,
    moment_gain_mlp,
    moment_query,
    moment_key,
    moment_value,
    moment_output,
    moment_gate,
    moment_up,
    moment_down,
):
    place = lax.axis_index("fsdp")
    far, near = place // 2, place % 2
    shard_rows = D // 4
    gains = jnp.stack([gain_attn, gain_mlp])
    gain_rows = jnp.pad(gains, ((0, 6), (0, 1024 - shard_rows)))
    pack_qkv = jnp.concatenate(
        [jnp.pad(jnp.concatenate([w_query, w_key, w_value], 1), ((0, 0), (0, 64))), gain_rows], 0
    )
    came_qkv = across(pack_qkv, "fsdp", 2)
    all_qkv = gather_shards(pack_qkv, came_qkv)
    shard_rest = jnp.concatenate([w_gate, w_up, w_output], 1)
    shard_rest, shard_down, unused = lax.optimization_barrier((shard_rest, w_down, came_qkv))
    came_rest = across(shard_rest, "fsdp", 2)
    came_down = across(shard_down, "fsdp", 2)
    full_qkv = all_qkv[:, :shard_rows].reshape(D, 1024)
    gain_first = all_qkv[:, shard_rows, :shard_rows].reshape(D).astype(wide)
    gain_second = all_qkv[:, shard_rows + 1, :shard_rows].reshape(D).astype(wide)
    full_rest = gather_shards(shard_rest, came_rest).reshape(D, -1)
    full_gate_up = full_rest[:, : 2 * FF]
    full_output = full_rest[:, 2 * FF :]
    full_down = gather_shards(shard_down, came_down).reshape(FF, D)
    tokens = hidden.shape[1]
    features = hidden[0].astype(wide)
    local_pos = positions[0]
    near_pos, far_pos = [
        half.reshape(-1, 1) for half in gather_context(local_pos.reshape(-1, 128))
    ]
    query_pos = jnp.tile(local_pos, H // KVH)[None, :]
    sequence_length = 2 * near_pos.shape[0]
    cosine, sine = angles(local_pos, HD)
    cosine = cosine[:, None, :]
    sine = sine[:, None, :]
    scale_first = lax.rsqrt(jnp.mean(features * features, axis=-1, keepdims=True) + epsilon)
    normed = (features * scale_first * gain_first).astype(low)
    qkv_pre = jnp.dot(normed, full_qkv, preferred_element_type=wide)
    query_pre = qkv_pre[:, :D]
    key_pre = qkv_pre[:, D : D + KV]
    value_pre = qkv_pre[:, D + KV : D + 2 * KV]
    query_rot = rotate(query_pre.reshape(tokens, H, HD), cosine, sine).astype(low)
    query_rot = query_rot.reshape(tokens, D)
    key_rot = rotate(key_pre.reshape(tokens, KVH, HD), cosine, sine).astype(low).reshape(tokens, KV)
    key_value = jnp.concatenate([key_rot, value_pre.astype(low)], 1)
    near_kv, far_kv = gather_context(key_value)

    state = attend(query_rot, near_kv, query_pos, near_pos)
    attended_low, attended, log_total = attend(query_rot, far_kv, query_pos, far_pos, state)
    mixed = features + jnp.dot(attended_low, full_output, preferred_element_type=wide)
    second_scale = lax.rsqrt(jnp.mean(mixed * mixed, axis=-1, keepdims=True) + epsilon)
    normed_mlp = (mixed * second_scale * gain_second).astype(low)
    gate_up = jnp.dot(normed_mlp, full_gate_up, preferred_element_type=wide)
    gate_pre = gate_up[:, :FF]
    up_pre = gate_up[:, FF:]
    inner = (jax.nn.silu(gate_pre) * up_pre).astype(low)
    result = mixed + jnp.dot(inner, full_down, preferred_element_type=wide)
    output = result.astype(low)[None]
    upstream_low = cotangent[0]
    upstream = upstream_low.astype(wide)
    grad_inner = jnp.einsum("td,fd->tf", upstream_low, full_down, preferred_element_type=wide)
    sigma = jax.nn.sigmoid(gate_pre)
    grad_up_pre = (grad_inner * gate_pre * sigma).astype(low)
    grad_gate_pre = (grad_inner * up_pre * sigma * (1.0 + gate_pre * (1.0 - sigma))).astype(low)
    grad_pre = jnp.concatenate([grad_gate_pre, grad_up_pre], 1)
    grad_normed_mlp = jnp.einsum("tf,df->td", grad_pre, full_gate_up, preferred_element_type=wide)
    gain_term_mlp = (grad_normed_mlp * mixed * second_scale).astype(low)
    inner_second = grad_normed_mlp * gain_second
    grad_mixed = (
        upstream
        + second_scale * inner_second
        - mixed * second_scale**3 * jnp.mean(inner_second * mixed, axis=-1, keepdims=True)
    )
    mixed_low = grad_mixed.astype(low)
    grad_gate_up = jnp.einsum("td,tf->df", normed_mlp, grad_pre, preferred_element_type=wide)
    grad_gate_up = grad_gate_up.astype(low)
    turned_down = jnp.einsum("td,tf->df", upstream_low, inner, preferred_element_type=wide)
    grad_out = jnp.einsum("td,te->de", attended_low, mixed_low, preferred_element_type=wide)
    even = jnp.stack([grad_gate_up[:, :FF], turned_down.astype(low)])
    odd = jnp.stack([grad_gate_up[:, FF:], jnp.pad(grad_out.astype(low), ((0, 0), (0, FF - D)))])
    kept = jnp.where(near == 0, even, odd)
    sent = jnp.where(near == 0, odd, even)
    chip = add(kept, across(sent, "fsdp", 1))
    own = add(pick(chip, far, 0), across(pick(chip, 1 - far, 0), "fsdp", 2))
    own_grad = reduce_context(own, 2)
    is_down = place == 2

    def by_shard(matrix):
        blocks = matrix.reshape(4, shard_rows, FF)
        return jnp.where(is_down, swap_blocks(blocks), blocks)

    moments_out = jnp.stack(
        [
            moment_gate.astype(low),
            moment_up.astype(low),
            columns_to_rows(moment_down.astype(low)),
            jnp.pad(moment_output.astype(low), ((0, 0), (0, FF - D))),
        ]
    )
    moments_out, unused = lax.optimization_barrier((moments_out, came_rest))
    own_old = exchange(moments_out)
    own_old = jnp.where(is_down, swap_blocks(own_old), own_old).reshape(D, FF)
    own_moment = momentum_decay * own_old.astype(wide) + own_grad.astype(wide)
    (own_orthogonal,) = orthogonalize(own_moment)
    grads_back = exchange(by_shard(own_grad))
    steps_back = exchange(by_shard(own_orthogonal))

    grad_attended = jnp.einsum("te,de->td", mixed_low, full_output, preferred_element_type=wide)
    grad_attended = grad_attended.astype(low)
    back = (query_rot, grad_attended, attended, log_total)
    begun, far_terms = attend_back(*back, far_kv, query_pos, far_pos)
    far_came = across(far_terms, "ctx", 1)
    grad_query_rot, near_terms = attend_back(*back, near_kv, query_pos, near_pos, begun)
    key_grads = scatter_context(near_terms, far_came)
    grad_query_pre = unrotate(grad_query_rot.reshape(tokens, H, HD), cosine, sine)
    grad_query_pre = grad_query_pre.reshape(tokens, D).astype(low)
    grad_query = jnp.einsum("td,te->de", normed, grad_query_pre, preferred_element_type=wide)
    total_query = reduce_rows(grad_query.astype(low))
    new_moment_query = momentum_decay * moment_query + total_query
    full_moment_query = gather_shards(new_moment_query.astype(low)).reshape(D, D).astype(wide)
    (orthogonal_query,) = orthogonalize(full_moment_query)
    grad_key_pre = unrotate(key_grads[:, :KV].reshape(tokens, KVH, HD), cosine, sine)
    grad_kv_pre = jnp.concatenate(
        [grad_key_pre.reshape(tokens, KV).astype(low), key_grads[:, KV:].astype(low)], 1
    )
    grad_qkv_pre = jnp.concatenate([grad_query_pre, grad_kv_pre], 1)
    grad_normed = jnp.einsum(
        "te,de->td", grad_qkv_pre, full_qkv[:, : D + 2 * KV], preferred_element_type=wide
    )
    inner_first = grad_normed * gain_first
    grad_hidden = (
        grad_mixed
        + scale_first * inner_first
        - features * scale_first**3 * jnp.mean(inner_first * features, axis=-1, keepdims=True)
    )
    gain_term = (grad_normed * features * scale_first).astype(low)
    ones = jnp.ones((tokens, 32), low)
    grad_kv = jnp.concatenate(
        [
            jnp.einsum("td,te->de", normed, grad_kv_pre, preferred_element_type=wide),
            jnp.einsum("td,te->de", gain_term, ones, preferred_element_type=wide),
            jnp.einsum("td,te->de", gain_term_mlp, ones, preferred_element_type=wide),
        ],
        1,
    )
    total_kv = reduce_rows(grad_kv.astype(low))

    def square_part(packed):
        return packed[:, :D]

    total_key = total_kv[:, :KV]
    total_value = total_kv[:, KV : 2 * KV]
    total_gain_attn = total_kv[:, 2 * KV]
    total_gain_mlp = total_kv[:, 2 * KV + 32]
    total_grads = (
        total_gain_attn,
        total_gain_mlp,
        total_query,
        total_key,
        total_value,
        square_part(grads_back[3]).astype(wide),
        grads_back[0].astype(wide),
        grads_back[1].astype(wide),
        rows_to_columns(grads_back[2]).astype(wide),
    )
    old_moments = (
        moment_gain_attn,
        moment_gain_mlp,
        moment_query,
        moment_key,
        moment_value,
        moment_output,
        moment_gate,
        moment_up,
        moment_down,
    )
    new_moments = tuple(
        (momentum_decay * old + fresh for old, fresh in zip(old_moments, total_grads))
    )
    small = jnp.concatenate([new_moments[3], new_moments[4]], 1).astype(low)
    small = gather_shards(small).reshape(D, 2 * KV)
    small, unused, unused = lax.optimization_barrier((small, own_orthogonal, orthogonal_query))
    small = small.astype(wide)
    orthogonal_key, orthogonal_value = orthogonalize(small[:, :KV], small[:, KV:])

    def rows_of(matrix):
        return lax.dynamic_slice_in_dim(matrix, place * shard_rows, shard_rows, 0)

    def stepped(weight, values, rows_total, cols_total):
        factor = math.sqrt(max(1.0, float(cols_total) / rows_total))
        return weight.astype(wide) - matrix_rate * factor * values.astype(wide)

    new_gate = stepped(w_gate, steps_back[0], D, FF)
    new_up = stepped(w_up, steps_back[1], D, FF)
    new_down = stepped(w_down, rows_to_columns(steps_back[2]), FF, D)
    new_output = stepped(w_output, square_part(steps_back[3]), D, D)
    new_query = stepped(w_query, rows_of(orthogonal_query), D, D)
    new_key = stepped(w_key, rows_of(orthogonal_key), D, KV)
    new_value = stepped(w_value, rows_of(orthogonal_value), D, KV)
    gain_step = gain_factor / math.sqrt(float(sequence_length * lax.axis_size("fsdp")))
    new_gain_attn = gain_attn.astype(wide) - gain_step * new_moments[0]
    new_gain_mlp = gain_mlp.astype(wide) - gain_step * new_moments[1]
    return (
        output,
        grad_hidden[None],
        *total_grads,
        *new_moments,
        new_gain_attn,
        new_gain_mlp,
        new_query,
        new_key,
        new_value,
        new_output,
        new_gate,
        new_up,
        new_down,
    )


def solution(mesh):
    return jax.shard_map(
        per_device,
        mesh=mesh,
        in_specs=(
            P("fsdp", "ctx", None),
            P("fsdp", "ctx"),
            P("fsdp", "ctx", None),
            P("fsdp"),
            P("fsdp"),
            P("fsdp", None),
            P("fsdp", None),
            P("fsdp", None),
            P("fsdp", None),
            P("fsdp", None),
            P("fsdp", None),
            P("fsdp", None),
            P("fsdp"),
            P("fsdp"),
            P("fsdp", None),
            P("fsdp", None),
            P("fsdp", None),
            P("fsdp", None),
            P("fsdp", None),
            P("fsdp", None),
            P("fsdp", None),
        ),
        out_specs=(
            P("fsdp", "ctx", None),
            P("fsdp", "ctx", None),
            P("fsdp"),
            P("fsdp"),
            P("fsdp", None),
            P("fsdp", None),
            P("fsdp", None),
            P("fsdp", None),
            P("fsdp", None),
            P("fsdp", None),
            P("fsdp", None),
            P("fsdp"),
            P("fsdp"),
            P("fsdp", None),
            P("fsdp", None),
            P("fsdp", None),
            P("fsdp", None),
            P("fsdp", None),
            P("fsdp", None),
            P("fsdp", None),
            P("fsdp"),
            P("fsdp"),
            P("fsdp", None),
            P("fsdp", None),
            P("fsdp", None),
            P("fsdp", None),
            P("fsdp", None),
            P("fsdp", None),
            P("fsdp", None),
        ),
        check_vma=False,
    )
```
